256 devices in a mesh: sec: 64 (over x, y_lo, z), tile: 4 (over y_hi, core).
Axes of the slice: x: 4, y: 4 (y_hi: 2, y_lo: 2; y = y_hi * 2 + y_lo), z: 8, core: 2. Of those that a mesh axis runs over, the one named last changes fastest.
Arguments:
- features: bfloat16 [64, 2048, 256], P('sec', 'tile'), may hold values from -16 to 16
- select: int32 [64, 2048], P('sec', 'tile'), may hold values from 1 to 7
- validity: int32 [64], P('sec'), may hold values 0 or 1
- offset_gain: float32 [3, 256], replicated, may hold values from 0.5 to 2
Outputs:
- aligned: bfloat16 [64, 2048, 256], P('sec', 'tile')
The draws below stay inside these ranges and needn't reach their ends.
Inputs may be any that keep to these rules, and one draw needn't show every extreme that they name: `select`: bit k - 1 of a value is 1 where offset k votes.
All inputs are finite; a program needn't handle non-finite values. No bound on the sum of `validity` on one device may be relied on, other than what follows from the above.
Results may differ from the reference program's by a relative error of at most 0.0027.
Values may be sent and summed in bfloat16 or wider, within the bound.
A program may use at most 64 MiB of HBM per device.

```python
import math
import jax
import jax.numpy as jnp
from jax import lax

CHANNELS = 256
POSITIONS = 2048
SECTIONS = 64


def draw_features(key, part):
    values_all = jax.random.normal(key, (SECTIONS, POSITIONS, CHANNELS), jnp.float32)
    return jnp.clip(values_all, -16.0, 16.0).astype(jnp.bfloat16)


def touch_ends(values, stream_key, low, top_value):
    longest = values.shape.index(max(values.shape))
    spots = []
    for shift in (0, 1):
        where = [jax.random.randint(jax.random.fold_in(stream_key, axis), (), 0, length) for axis, length in enumerate(values.shape)]
        where[longest] = (where[longest] + shift) % values.shape[longest]
        spots.append(tuple(where))
    return values.at[spots[0]].set(low).at[spots[1]].set(top_value)


def setup_inputs(seed: int = 0) -> dict:
    keys = jax.random.split(jax.random.key(seed), 5)
    return {
        "features": draw_features(jax.random.fold_in(keys[4], 71), 0),
        "select": touch_ends(jax.random.randint(keys[1], (SECTIONS, POSITIONS), 1, 8), jax.random.fold_in(keys[1], 1), 1, 7).astype(jnp.int32),
        "validity": touch_ends((jax.random.randint(keys[2], (SECTIONS,), 0, 4) < 3).astype(jnp.int32), jax.random.fold_in(keys[2], 1), 0, 1),
        "offset_gain": jnp.clip(jnp.exp(jax.random.uniform(keys[3], (3, CHANNELS), jnp.float32, math.log(0.5), math.log(2.0))), 0.5, 2.0),
    }


score_factor = 2.5

def match_section(queries, key_rows):
    score_scale = score_factor / math.sqrt(key_rows.shape[-1])
    scores = jnp.dot(queries, key_rows.T, preferred_element_type=jnp.float32) * score_scale
    row_max = lax.optimization_barrier(jnp.max(scores, axis=1))
    weights = jnp.exp(scores - row_max[:, None])
    row_sum = lax.optimization_barrier(jnp.sum(weights, axis=1))
    weighted = jnp.dot(weights.astype(jnp.bfloat16), key_rows, preferred_element_type=jnp.float32)
    return weighted / row_sum[:, None]

def reference(features, select, validity, offset_gain):

    def per_section(section_id):
        queries = lax.dynamic_index_in_dim(features, section_id, 0, keepdims=False)
        selection = lax.dynamic_index_in_dim(select, section_id, 0, keepdims=False)
        numerator = jnp.zeros((queries.shape[0], queries.shape[1]), jnp.float32)
        vote_count = jnp.zeros((queries.shape[0],), jnp.float32)
        for offset in range(1, 4):
            source = jnp.maximum(section_id - offset, 0).astype(jnp.int32)
            key_rows = lax.dynamic_index_in_dim(features, source, 0, keepdims=False)
            usable = jnp.where(section_id - offset >= 0, validity[source], 0).astype(jnp.float32)
            chosen = (selection // 2 ** (offset - 1) % 2).astype(jnp.float32) * usable
            warped = match_section(queries, key_rows)
            numerator = numerator + chosen[:, None] * offset_gain[offset - 1][None, :] * warped
            vote_count = vote_count + chosen
        return (numerator / jnp.maximum(vote_count, 1.0)[:, None]).astype(jnp.bfloat16)
    return lax.map(per_section, jnp.arange(SECTIONS, dtype=jnp.int32))
```

```python
import functools
import math

import jax
import jax.numpy as jnp
from jax import lax
from jax.experimental import pallas as pl
from jax.experimental.pallas import tpu as pltpu
from jax.sharding import PartitionSpec as P

MESH = pl.DeviceIdType.MESH
OFFSETS = 3
LENGTH_Z = 8
LENGTH_Y = 4
LENGTH_X = 4
PIECES = 4
SLOTS = 5
ROW_BLOCK = 256
score_factor = 2.5


def device_at(x, y, z, core):
    return ((x * 2 + y % 2) * LENGTH_Z + z, (y // 2) * 2 + core)


def kernel(
    features,
    select,
    validity,
    gain,
    out,
    keys,
    queries,
    votes_in,
    gains,
    own_flag,
    flags,
    high,
    total,
    weighted,
    chosen,
    numerator,
    local_sem,
    arrive,
    sent_up,
    sent_side,
    sent_core,
    flag_arrive,
    flag_sent,
):
    rows, channels = queries.shape
    ticks = OFFSETS * PIECES
    piece = rows // PIECES
    to_exponent = score_factor / math.sqrt(channels) * math.log2(math.e)

    section, tile = lax.axis_index("sec"), lax.axis_index("tile")
    z = section % LENGTH_Z
    x = section // (2 * LENGTH_Z)
    y = (tile // 2) * 2 + (section // LENGTH_Z) % 2
    core = tile % 2
    first = z == 0
    odd = y % 2
    last_z = z == LENGTH_Z - 1

    up = device_at(
        jnp.where(last_z, (x + odd) % LENGTH_X, x), y, (z + 1) % LENGTH_Z, core
    )
    down = device_at(
        jnp.where(first, (x + LENGTH_X - odd) % LENGTH_X, x), y, (z + LENGTH_Z - 1) % LENGTH_Z, core
    )
    partner = device_at(x, y, z, 1 - core)
    pair = device_at(x, (y + 2) % LENGTH_Y, z, core)
    right = device_at(x, (y + 1) % LENGTH_Y, z, core)
    left = device_at(x, (y + 3) % LENGTH_Y, z, core)

    copy_queries = pltpu.make_async_copy(features.at[0], queries, local_sem.at[0])
    copy_votes = pltpu.make_async_copy(select, votes_in, local_sem.at[1])
    copy_gains = pltpu.make_async_copy(gain, gains, local_sem.at[2])
    copy_flag = pltpu.make_async_copy(validity, own_flag, local_sem.at[3])
    copy_flag.start()
    copy_queries.start()
    copy_votes.start()
    copy_gains.start()

    barrier = pltpu.get_barrier_semaphore()

    def greet(target):
        pl.semaphore_signal(barrier, inc=1, device_id=target, device_id_type=MESH)

    greet(down)
    greet(partner)

    @pl.when(first)
    def _():
        greet(left)
        greet(right)
        pl.semaphore_wait(barrier, 4)

    @pl.when(jnp.logical_not(first))
    def _():
        greet(pair)
        pl.semaphore_wait(barrier, 3)

    def send(source, tick, slot, sem, target):
        return pltpu.make_async_remote_copy(
            src_ref=source,
            dst_ref=keys.at[tick, slot],
            send_sem=sem,
            recv_sem=arrive.at[tick, slot],
            device_id=target,
            device_id_type=MESH,
        )

    def own_piece(j):
        return features.at[0, pl.ds(j * piece, piece)]

    def send_flag(source, slot, sem, target):
        return pltpu.make_async_remote_copy(
            src_ref=source,
            dst_ref=flags.at[slot],
            send_sem=sem,
            recv_sem=flag_arrive.at[slot],
            device_id=target,
            device_id_type=MESH,
        )

    def send_own_flag():
        return send_flag(own_flag, 0, flag_sent.at[0], up)

    for j in range(PIECES):
        send(own_piece(j), j, 0, sent_up.at[j], up).start()
    copy_flag.wait()
    send_own_flag().start()
    copy_queries.wait()
    copy_votes.wait()
    copy_gains.wait()

    numerator[...] = jnp.zeros_like(numerator)

    def wait_for(tick, slot):
        pltpu.make_async_copy(keys.at[tick, slot], keys.at[tick, slot], arrive.at[tick, slot]).wait()

    def relay_up(i, slot):
        return send(keys.at[i, slot], i + PIECES, 0, sent_up.at[i + PIECES], up)

    def to_pair(i):
        return send(keys.at[i, 0], i, 1, sent_side.at[0, i], pair)

    def to_right(i):
        return send(keys.at[i, 0], i, 4, sent_side.at[0, i], right)

    def to_left(i):
        return send(keys.at[i, 0], i, 1, sent_side.at[1, i], left)

    def to_core(i, source, slot):
        return send(keys.at[i, source], i, slot, sent_core.at[slot - 2, i], partner)

    def take_from_below(i):
        wait_for(i, 0)

        @pl.when(first)
        def _():
            to_right(i).start()
            to_left(i).start()

        @pl.when(jnp.logical_not(first))
        def _():
            @pl.when(i < ticks - PIECES)
            def _():
                relay_up(i, 0).start()

            to_pair(i).start()
            to_core(i, 0, 2).start()

    def take_from_side(i):
        @pl.when(first)
        def _():
            wait_for(i, 4)

            @pl.when(i < ticks - PIECES)
            def _():
                relay_up(i, 4).start()

            to_core(i, 4, 2).start()

        wait_for(i, 1)
        to_core(i, 1, 3).start()

    start = jnp.where(first, 1, 0)

    def match(i):
        wait_for(i, 2)
        wait_for(i, 3)
        offset = i // PIECES

        @pl.when(i % PIECES == 0)
        def _():
            high[...] = jnp.full_like(high, -1e30)
            total[...] = jnp.zeros_like(total)
            weighted[...] = jnp.zeros_like(weighted)

        for block in range(rows // ROW_BLOCK):
            part = pl.ds(block * ROW_BLOCK, ROW_BLOCK)
            key_rows = keys[i, pl.ds(start, 4)].reshape(4 * piece, channels)
            scores = lax.dot_general(
                queries[part], key_rows, (((1,), (1,)), ((), ())), preferred_element_type=jnp.float32
            )
            before = high[part]
            now = jnp.maximum(before, jnp.max(scores, axis=1, keepdims=True) * to_exponent)
            weights = jnp.exp2(scores * to_exponent - now[:, :1])
            fade = jnp.exp2(before - now)
            partial = weights[:, :128]
            for lane in range(128, 4 * piece, 128):
                partial = partial + weights[:, lane : lane + 128]
            total[part] = fade * total[part] + partial
            weighted[part] = jnp.concatenate([fade, fade], axis=1) * weighted[part] + jnp.dot(
                weights.astype(jnp.bfloat16), key_rows, preferred_element_type=jnp.float32
            )
            high[part] = now

        @pl.when(i % PIECES == PIECES - 1)
        def _():
            vote = chosen[pl.ds(offset, 1)][0]
            factor = vote[:, :1] / jnp.sum(total[...], axis=1, keepdims=True)
            numerator[...] += factor * gains[pl.ds(offset, 1)] * weighted[...]

    picks = jnp.broadcast_to(votes_in[...], (128, rows)).T

    def flag_wait(slot):
        pltpu.make_async_copy(flags.at[slot], flags.at[slot], flag_arrive.at[slot]).wait()

    def relay_flag(offset):
        @pl.when(first)
        def _():
            flag_wait(offset)
            send_flag(flags.at[offset], 3 + offset, flag_sent.at[3 + offset], right).start()
            flag_wait(3 + offset)
            if offset < OFFSETS - 1:
                send_flag(flags.at[3 + offset], offset + 1, flag_sent.at[offset + 1], up).start()

        @pl.when(jnp.logical_not(first))
        def _():
            flag_wait(offset)
            if offset < OFFSETS - 1:
                send_flag(flags.at[offset], offset + 1, flag_sent.at[offset + 1], up).start()

    def vote_of(offset):
        usable = flags[jnp.where(first, 3 + offset, offset), 0]
        usable = jnp.where(section >= offset + 1, usable, 0).astype(jnp.float32)
        return (picks // 2**offset % 2).astype(jnp.float32) * usable

    def step(i, carry):
        @pl.when(i < ticks)
        def _():
            take_from_below(i)

        @pl.when(jnp.logical_and(i >= 2, i < ticks + 2))
        def _():
            take_from_side(i - 2)

        for offset in range(OFFSETS):
            @pl.when(i == offset * PIECES + 2)
            def _():
                relay_flag(offset)
                chosen[offset] = vote_of(offset)

        @pl.when(i >= 3)
        def _():
            match(i - 3)

        return carry

    lax.fori_loop(0, ticks + 3, step, 0)

    count = chosen[0] + chosen[1] + chosen[2]
    out[0] = (numerator[...] / jnp.maximum(count, 1.0)[:, :1]).astype(jnp.bfloat16)

    def finish(i, carry):
        @pl.when(i < PIECES)
        def _():
            send(own_piece(i), i, 0, sent_up.at[i], up).wait_send()

        @pl.when(first)
        def _():
            @pl.when(i < ticks - PIECES)
            def _():
                relay_up(i, 4).wait_send()

            to_right(i).wait_send()
            to_left(i).wait_send()
            to_core(i, 4, 2).wait_send()

        @pl.when(jnp.logical_not(first))
        def _():
            @pl.when(i < ticks - PIECES)
            def _():
                relay_up(i, 0).wait_send()

            to_pair(i).wait_send()
            to_core(i, 0, 2).wait_send()

        to_core(i, 1, 3).wait_send()
        return carry

    lax.fori_loop(0, ticks, finish, 0)
    send_own_flag().wait_send()
    for offset in range(OFFSETS):
        @pl.when(first)
        def _():
            send_flag(flags.at[offset], 3 + offset, flag_sent.at[3 + offset], right).wait_send()

        if offset < OFFSETS - 1:
            send_flag(flags.at[offset], offset + 1, flag_sent.at[offset + 1], up).wait_send()


def shards(features, select, validity, offset_gain):
    rows, channels = features.shape[1:]
    ticks = OFFSETS * PIECES
    anywhere = pl.BlockSpec(memory_space=pl.ANY)
    dma = pltpu.SemaphoreType.DMA
    return pl.pallas_call(
        kernel,
        out_shape=jax.ShapeDtypeStruct(features.shape, jnp.bfloat16),
        in_specs=[anywhere] * 4,
        out_specs=pl.BlockSpec(memory_space=pltpu.VMEM),
        scratch_shapes=[
            pltpu.VMEM((ticks, SLOTS, rows // PIECES, channels), jnp.bfloat16),
            pltpu.VMEM((rows, channels), jnp.bfloat16),
            pltpu.VMEM(select.shape, jnp.int32),
            pltpu.VMEM(offset_gain.shape, jnp.float32),
            pltpu.SMEM((1,), jnp.int32),
            pltpu.SMEM((2 * OFFSETS, 1), jnp.int32),
            pltpu.VMEM((rows, 128), jnp.float32),
            pltpu.VMEM((rows, 128), jnp.float32),
            pltpu.VMEM((rows, channels), jnp.float32),
            pltpu.VMEM((OFFSETS, rows, 128), jnp.float32),
            pltpu.VMEM((rows, channels), jnp.float32),
            dma((4,)),
            dma((ticks, SLOTS)),
            dma((ticks,)),
            dma((2, ticks)),
            dma((2, ticks)),
            dma((2 * OFFSETS,)),
            dma((2 * OFFSETS,)),
        ],
        compiler_params=pltpu.CompilerParams(collective_id=0, has_side_effects=True),
    )(features, select, validity, offset_gain)


def solution(mesh):
    in_specs = (P("sec", "tile", None), P("sec", "tile"), P("sec"), P())
    out_specs = P("sec", "tile", None)
    return jax.shard_map(shards, mesh=mesh, in_specs=in_specs, out_specs=out_specs, check_vma=False)
```

```python
import functools
import math

import jax
import jax.numpy as jnp
from jax import lax
from jax.experimental import pallas as pl
from jax.experimental.pallas import tpu as pltpu
from jax.sharding import PartitionSpec as P

MESH = pl.DeviceIdType.MESH
OFFSETS = 3
LENGTH_Z = 8
LENGTH_Y = 4
LENGTH_X = 4
PIECES = 8
GROUP = 2
SIDE_LAG = 6
MATCH_LAG = 8
SLOTS = 5
ROW_BLOCK = 256
score_factor = 2.5


def device_at(x, y, z, core):
    return ((x * 2 + y % 2) * LENGTH_Z + z, (y // 2) * 2 + core)


def kernel(
    features,
    select,
    validity,
    gain,
    out,
    keys,
    queries,
    votes_in,
    gains,
    own_flag,
    flags,
    high,
    total,
    weighted,
    chosen,
    numerator,
    count,
    local_sem,
    arrive,
    sent,
    flag_arrive,
    flag_sent,
):
    rows, channels = queries.shape
    ticks = OFFSETS * PIECES
    groups = PIECES // GROUP
    sections = lax.axis_size("sec")
    piece = rows // PIECES
    to_exponent = score_factor / math.sqrt(channels) * math.log2(math.e)

    section, tile = lax.axis_index("sec"), lax.axis_index("tile")
    z = section % LENGTH_Z
    x = section // (2 * LENGTH_Z)
    y = (tile // 2) * 2 + (section // LENGTH_Z) % 2
    core = tile % 2
    first = z == 0
    odd = y % 2
    last_z = z == LENGTH_Z - 1

    up = device_at(
        jnp.where(last_z, (x + odd) % LENGTH_X, x), y, (z + 1) % LENGTH_Z, core
    )
    down = device_at(
        jnp.where(first, (x + LENGTH_X - odd) % LENGTH_X, x), y, (z + LENGTH_Z - 1) % LENGTH_Z, core
    )
    partner = device_at(x, y, z, 1 - core)
    pair = device_at(x, (y + 2) % LENGTH_Y, z, core)
    right = device_at(x, (y + 1) % LENGTH_Y, z, core)
    left = device_at(x, (y + 3) % LENGTH_Y, z, core)

    copy_queries = pltpu.make_async_copy(features.at[0], queries, local_sem.at[0])
    copy_votes = pltpu.make_async_copy(select, votes_in, local_sem.at[1])
    copy_gains = pltpu.make_async_copy(gain, gains, local_sem.at[2])
    copy_flag = pltpu.make_async_copy(validity, own_flag, local_sem.at[3])
    copy_flag.start()
    copy_queries.start()
    copy_votes.start()
    copy_gains.start()

    barrier = pltpu.get_barrier_semaphore()

    def greet(target):
        pl.semaphore_signal(barrier, inc=1, device_id=target, device_id_type=MESH)

    greet(down)
    greet(partner)
    for offset in range(OFFSETS):
        greet(((section + sections - offset - 1) % sections, tile))

    @pl.when(first)
    def _():
        greet(left)
        greet(right)

    @pl.when(jnp.logical_not(first))
    def _():
        greet(pair)

    copy_votes.wait()
    copy_gains.wait()
    picks = jnp.broadcast_to(votes_in[...], (128, rows)).T
    for offset in range(OFFSETS):
        chosen[offset] = (picks // 2**offset % 2).astype(jnp.float32)
    numerator[...] = jnp.zeros_like(numerator)
    count[...] = jnp.zeros_like(count)
    pl.semaphore_wait(barrier, 3 + OFFSETS + jnp.where(first, 1, 0))

    def send(source, tick, slot, sem, target):
        return pltpu.make_async_remote_copy(
            src_ref=source,
            dst_ref=keys.at[tick, slot],
            send_sem=sem,
            recv_sem=arrive.at[tick, slot],
            device_id=target,
            device_id_type=MESH,
        )

    def own_piece(j):
        return features.at[0, pl.ds(j * piece, piece)]

    def send_flag(offset):
        return pltpu.make_async_remote_copy(
            src_ref=own_flag,
            dst_ref=flags.at[offset],
            send_sem=flag_sent.at[offset],
            recv_sem=flag_arrive.at[offset],
            device_id=((section + offset + 1) % sections, tile),
            device_id_type=MESH,
        )

    copy_flag.wait()
    for offset in range(OFFSETS):
        send_flag(offset).start()
    for j in range(PIECES):
        send(own_piece(j), j, 0, sent, up).start()
    copy_queries.wait()

    def wait_for(tick, slot):
        pltpu.make_async_copy(keys.at[tick, slot], keys.at[tick, slot], arrive.at[tick, slot]).wait()

    def relay_up(i, slot):
        return send(keys.at[i, slot], i + PIECES, 0, sent, up)

    def to_pair(i):
        return send(keys.at[i, 0], i, 1, sent, pair)

    def to_right(i):
        return send(keys.at[i, 0], i, 4, sent, right)

    def to_left(i):
        return send(keys.at[i, 0], i, 1, sent, left)

    def to_core(i, source, slot):
        return send(keys.at[i, source], i, slot, sent, partner)

    def take_from_below(i):
        wait_for(i, 0)

        @pl.when(first)
        def _():
            to_right(i).start()
            to_left(i).start()

        @pl.when(jnp.logical_not(first))
        def _():
            @pl.when(i < ticks - PIECES)
            def _():
                relay_up(i, 0).start()

            to_pair(i).start()
            to_core(i, 0, 2).start()

    def take_from_side(i):
        @pl.when(first)
        def _():
            wait_for(i, 4)

            @pl.when(i < ticks - PIECES)
            def _():
                relay_up(i, 4).start()

            to_core(i, 4, 2).start()

        wait_for(i, 1)
        to_core(i, 1, 3).start()

    start = jnp.where(first, 1, 0)

    def match(g):
        for k in range(GROUP):
            wait_for(g * GROUP + k, 2)
            wait_for(g * GROUP + k, 3)
        offset = g // groups

        @pl.when(g % groups == 0)
        def _():
            high[...] = jnp.full_like(high, -1e30)
            total[...] = jnp.zeros_like(total)
            weighted[...] = jnp.zeros_like(weighted)

        for block in range(rows // ROW_BLOCK):
            part = pl.ds(block * ROW_BLOCK, ROW_BLOCK)
            key_rows = keys[pl.ds(g * GROUP, GROUP), pl.ds(start, 4)].reshape(GROUP * 4 * piece, channels)
            scores = lax.dot_general(
                queries[part], key_rows, (((1,), (1,)), ((), ())), preferred_element_type=jnp.float32
            )
            before = high[part]
            now = jnp.maximum(before, jnp.max(scores, axis=1, keepdims=True) * to_exponent)
            weights = jnp.exp2(scores * to_exponent - now[:, :1])
            fade = jnp.exp2(before - now)
            partial = weights[:, :128]
            for lane in range(128, GROUP * 4 * piece, 128):
                partial = partial + weights[:, lane : lane + 128]
            total[part] = fade * total[part] + partial
            weighted[part] = jnp.concatenate([fade, fade], axis=1) * weighted[part] + jnp.dot(
                weights.astype(jnp.bfloat16), key_rows, preferred_element_type=jnp.float32
            )
            high[part] = now

        @pl.when(g % groups == groups - 1)
        def _():
            pltpu.make_async_copy(flags.at[offset], flags.at[offset], flag_arrive.at[offset]).wait()
            usable = jnp.where(section > offset, flags[offset, 0], 0).astype(jnp.float32)
            vote = chosen[pl.ds(offset, 1)][0] * usable
            count[...] += vote
            factor = vote[:, :1] / jnp.sum(total[...], axis=1, keepdims=True)
            numerator[...] += factor * gains[pl.ds(offset, 1)] * weighted[...]

    def step(i, carry):
        @pl.when(i < ticks)
        def _():
            take_from_below(i)

        @pl.when(jnp.logical_and(i >= SIDE_LAG, i < ticks + SIDE_LAG))
        def _():
            take_from_side(i - SIDE_LAG)

        @pl.when(jnp.logical_and(i >= MATCH_LAG + GROUP - 1, (i - MATCH_LAG) % GROUP == GROUP - 1))
        def _():
            match((i - MATCH_LAG) // GROUP)

        return carry

    lax.fori_loop(0, ticks + MATCH_LAG, step, 0)

    out[0] = (numerator[...] / jnp.maximum(count[...], 1.0)[:, :1]).astype(jnp.bfloat16)

    def wait_sent(slots):
        everything = keys.at[:, pl.ds(0, slots)]
        pltpu.make_async_copy(everything, everything, sent).wait()

    @pl.when(first)
    def _():
        wait_sent(5)

    @pl.when(jnp.logical_not(first))
    def _():
        wait_sent(4)

    for offset in range(OFFSETS):
        send_flag(offset).wait_send()


def shards(features, select, validity, offset_gain):
    rows, channels = features.shape[1:]
    ticks = OFFSETS * PIECES
    anywhere = pl.BlockSpec(memory_space=pltpu.HBM)
    dma = pltpu.SemaphoreType.DMA
    return pl.pallas_call(
        kernel,
        out_shape=jax.ShapeDtypeStruct(features.shape, jnp.bfloat16),
        in_specs=[anywhere] * 4,
        out_specs=pl.BlockSpec(memory_space=pltpu.VMEM),
        scratch_shapes=[
            pltpu.VMEM((ticks, SLOTS, rows // PIECES, channels), jnp.bfloat16),
            pltpu.VMEM((rows, channels), jnp.bfloat16),
            pltpu.VMEM(select.shape, jnp.int32),
            pltpu.VMEM(offset_gain.shape, jnp.float32),
            pltpu.SMEM((1,), jnp.int32),
            pltpu.SMEM((OFFSETS, 1), jnp.int32),
            pltpu.VMEM((rows, 128), jnp.float32),
            pltpu.VMEM((rows, 128), jnp.float32),
            pltpu.VMEM((rows, channels), jnp.float32),
            pltpu.VMEM((OFFSETS, rows, 128), jnp.float32),
            pltpu.VMEM((rows, channels), jnp.float32),
            pltpu.VMEM((rows, 128), jnp.float32),
            dma((4,)),
            dma((ticks, SLOTS)),
            dma,
            dma((OFFSETS,)),
            dma((OFFSETS,)),
        ],
        compiler_params=pltpu.CompilerParams(collective_id=0, has_side_effects=True),
    )(features, select, validity, offset_gain)


def solution(mesh):
    in_specs = (P("sec", "tile", None), P("sec", "tile"), P("sec"), P())
    out_specs = P("sec", "tile", None)
    return jax.shard_map(shards, mesh=mesh, in_specs=in_specs, out_specs=out_specs, check_vma=False)
```

```python
import functools
import math

import jax
import jax.numpy as jnp
from jax import lax
from jax.experimental import pallas as pl
from jax.experimental.pallas import tpu as pltpu
from jax.sharding import PartitionSpec as P

MESH = pl.DeviceIdType.MESH
OFFSETS = 3
LENGTH_Z = 8
LENGTH_Y = 4
LENGTH_X = 4
PIECES = 8
GROUP = 2
SIDE_LAG = 6
MATCH_LAG = 8
SLOTS = 5
ROW_BLOCK = 256
score_factor = 2.5


def device_at(x, y, z, core):
    return ((x * 2 + y % 2) * LENGTH_Z + z, (y // 2) * 2 + core)


def kernel(
    features,
    select,
    validity,
    gain,
    out,
    keys,
    queries,
    votes_in,
    gains,
    own_flag,
    flags,
    high,
    total,
    weighted,
    chosen,
    numerator,
    count,
    local_sem,
    arrive,
    sent,
    flag_arrive,
    flag_sent,
):
    rows, channels = queries.shape
    ticks = OFFSETS * PIECES
    groups = PIECES // GROUP
    sections = lax.axis_size("sec")
    piece = rows // PIECES
    to_exponent = score_factor / math.sqrt(channels) * math.log2(math.e)

    section, tile = lax.axis_index("sec"), lax.axis_index("tile")
    z = section % LENGTH_Z
    x = section // (2 * LENGTH_Z)
    y = (tile // 2) * 2 + (section // LENGTH_Z) % 2
    core = tile % 2
    first = z == 0
    odd = y % 2
    last_z = z == LENGTH_Z - 1
    sends_up = section < sections - 1

    def crosses(offset):
        return offset >= z

    def comes_up(offset):
        return jnp.logical_not(jnp.logical_and(jnp.logical_and(x == 0, odd == 1), crosses(offset)))

    def usable_offset(offset):
        return section > offset

    up = device_at(
        jnp.where(last_z, (x + odd) % LENGTH_X, x), y, (z + 1) % LENGTH_Z, core
    )
    down = device_at(
        jnp.where(first, (x + LENGTH_X - odd) % LENGTH_X, x), y, (z + LENGTH_Z - 1) % LENGTH_Z, core
    )
    partner = device_at(x, y, z, 1 - core)
    pair = device_at(x, (y + 2) % LENGTH_Y, z, core)
    right = device_at(x, (y + 1) % LENGTH_Y, z, core)
    left = device_at(x, (y + 3) % LENGTH_Y, z, core)

    copy_queries = pltpu.make_async_copy(features.at[0], queries, local_sem.at[0])
    copy_votes = pltpu.make_async_copy(select, votes_in, local_sem.at[1])
    copy_gains = pltpu.make_async_copy(gain, gains, local_sem.at[2])
    copy_flag = pltpu.make_async_copy(validity, own_flag, local_sem.at[3])
    copy_flag.start()
    copy_queries.start()
    copy_votes.start()
    copy_gains.start()

    barrier = pltpu.get_barrier_semaphore()

    def greet(target):
        pl.semaphore_signal(barrier, inc=1, device_id=target, device_id_type=MESH)

    greet(down)
    greet(partner)
    for offset in range(OFFSETS):
        greet(((section + sections - offset - 1) % sections, tile))

    @pl.when(z < OFFSETS)
    def _():
        greet(left)
        greet(right)

    @pl.when(z > 0)
    def _():
        greet(pair)

    copy_votes.wait()
    copy_gains.wait()
    picks = jnp.broadcast_to(votes_in[...], (128, rows)).T
    for offset in range(OFFSETS):
        chosen[offset] = (picks // 2**offset % 2).astype(jnp.float32)
    numerator[...] = jnp.zeros_like(numerator)
    count[...] = jnp.zeros_like(count)
    pl.semaphore_wait(barrier, 2 + OFFSETS + jnp.where(z < OFFSETS, 2, 0) + jnp.where(z > 0, 1, 0))

    def send(source, tick, slot, sem, target):
        return pltpu.make_async_remote_copy(
            src_ref=source,
            dst_ref=keys.at[tick, slot],
            send_sem=sem,
            recv_sem=arrive.at[tick, slot],
            device_id=target,
            device_id_type=MESH,
        )

    def own_piece(j):
        return features.at[0, pl.ds(j * piece, piece)]

    def send_flag(offset):
        return pltpu.make_async_remote_copy(
            src_ref=own_flag,
            dst_ref=flags.at[offset],
            send_sem=flag_sent.at[offset],
            recv_sem=flag_arrive.at[offset],
            device_id=((section + offset + 1) % sections, tile),
            device_id_type=MESH,
        )

    copy_flag.wait()
    for offset in range(OFFSETS):
        send_flag(offset).start()

    @pl.when(sends_up)
    def _():
        for j in range(PIECES):
            send(own_piece(j), j, 0, sent.at[0, 0], up).start()

    copy_queries.wait()

    def wait_for(tick, slot):
        pltpu.make_async_copy(keys.at[tick, slot], keys.at[tick, slot], arrive.at[tick, slot]).wait()

    def take_from_below(i):
        offset = i // PIECES

        @pl.when(comes_up(offset))
        def _():
            wait_for(i, 0)

            @pl.when(jnp.logical_and(sends_up, offset < OFFSETS - 1))
            def _():
                send(keys.at[i, 0], i + PIECES, 0, sent.at[0, offset + 1], up).start()

            @pl.when(crosses(offset))
            def _():
                send(keys.at[i, 0], i, 4, sent.at[1, offset], right).start()
                send(keys.at[i, 0], i, 1, sent.at[2, offset], left).start()

            @pl.when(jnp.logical_not(crosses(offset)))
            def _():
                send(keys.at[i, 0], i, 1, sent.at[1, offset], pair).start()
                send(keys.at[i, 0], i, 2, sent.at[3, offset], partner).start()

    def take_from_side(i):
        offset = i // PIECES

        @pl.when(usable_offset(offset))
        def _():
            @pl.when(crosses(offset))
            def _():
                wait_for(i, 4)
                send(keys.at[i, 4], i, 2, sent.at[3, offset], partner).start()

            wait_for(i, 1)
            send(keys.at[i, 1], i, 3, sent.at[4, offset], partner).start()

    def flag_wait(offset):
        pltpu.make_async_copy(flags.at[offset], flags.at[offset], flag_arrive.at[offset]).wait()

    def match(g):
        for k in range(GROUP):
            wait_for(g * GROUP + k, 2)
            wait_for(g * GROUP + k, 3)
        offset = g // groups
        start = jnp.where(crosses(offset), 1, 0)

        @pl.when(g % groups == 0)
        def _():
            high[...] = jnp.full_like(high, -1e30)
            total[...] = jnp.zeros_like(total)
            weighted[...] = jnp.zeros_like(weighted)

        for block in range(rows // ROW_BLOCK):
            part = pl.ds(block * ROW_BLOCK, ROW_BLOCK)
            key_rows = keys[pl.ds(g * GROUP, GROUP), pl.ds(start, 4)].reshape(GROUP * 4 * piece, channels)
            scores = lax.dot_general(
                queries[part], key_rows, (((1,), (1,)), ((), ())), preferred_element_type=jnp.float32
            )
            before = high[part]
            now = jnp.maximum(before, jnp.max(scores, axis=1, keepdims=True) * to_exponent)
            weights = jnp.exp2(scores * to_exponent - now[:, :1])
            fade = jnp.exp2(before - now)
            partial = weights[:, :128]
            for lane in range(128, GROUP * 4 * piece, 128):
                partial = partial + weights[:, lane : lane + 128]
            total[part] = fade * total[part] + partial
            weighted[part] = jnp.concatenate([fade, fade], axis=1) * weighted[part] + jnp.dot(
                weights.astype(jnp.bfloat16), key_rows, preferred_element_type=jnp.float32
            )
            high[part] = now

        @pl.when(g % groups == groups - 1)
        def _():
            flag_wait(offset)
            usable = flags[offset, 0].astype(jnp.float32)
            vote = chosen[pl.ds(offset, 1)][0] * usable
            count[...] += vote
            factor = vote[:, :1] / jnp.sum(total[...], axis=1, keepdims=True)
            numerator[...] += factor * gains[pl.ds(offset, 1)] * weighted[...]

    def step(i, carry):
        @pl.when(i < ticks)
        def _():
            take_from_below(i)

        @pl.when(jnp.logical_and(i >= SIDE_LAG, i < ticks + SIDE_LAG))
        def _():
            take_from_side(i - SIDE_LAG)

        @pl.when(jnp.logical_and(i >= MATCH_LAG + GROUP - 1, (i - MATCH_LAG) % GROUP == GROUP - 1))
        def _():
            g = (i - MATCH_LAG) // GROUP

            @pl.when(usable_offset(g // groups))
            def _():
                match(g)

        return carry

    lax.fori_loop(0, ticks + MATCH_LAG, step, 0)

    out[0] = (numerator[...] / jnp.maximum(count[...], 1.0)[:, :1]).astype(jnp.bfloat16)

    def wait_sent(kind, offset, sends):
        @pl.when(sends)
        def _():
            tile_sent = keys.at[pl.ds(0, PIECES), 0]
            pltpu.make_async_copy(tile_sent, tile_sent, sent.at[kind, offset]).wait()

    wait_sent(0, 0, sends_up)
    for offset in range(OFFSETS):
        if offset > 0:
            wait_sent(0, offset, jnp.logical_and(sends_up, comes_up(offset - 1)))
        wait_sent(1, offset, comes_up(offset))
        wait_sent(2, offset, jnp.logical_and(comes_up(offset), crosses(offset)))
        wait_sent(3, offset, usable_offset(offset))
        wait_sent(4, offset, usable_offset(offset))

    for offset in range(OFFSETS):
        @pl.when(jnp.logical_not(usable_offset(offset)))
        def _():
            flag_wait(offset)

        send_flag(offset).wait_send()


def shards(features, select, validity, offset_gain):
    rows, channels = features.shape[1:]
    ticks = OFFSETS * PIECES
    anywhere = pl.BlockSpec(memory_space=pltpu.HBM)
    dma = pltpu.SemaphoreType.DMA
    return pl.pallas_call(
        kernel,
        out_shape=jax.ShapeDtypeStruct(features.shape, jnp.bfloat16),
        in_specs=[anywhere] * 4,
        out_specs=pl.BlockSpec(memory_space=pltpu.VMEM),
        scratch_shapes=[
            pltpu.VMEM((ticks, SLOTS, rows // PIECES, channels), jnp.bfloat16),
            pltpu.VMEM((rows, channels), jnp.bfloat16),
            pltpu.VMEM(select.shape, jnp.int32),
            pltpu.VMEM(offset_gain.shape, jnp.float32),
            pltpu.SMEM((1,), jnp.int32),
            pltpu.SMEM((OFFSETS, 1), jnp.int32),
            pltpu.VMEM((rows, 128), jnp.float32),
            pltpu.VMEM((rows, 128), jnp.float32),
            pltpu.VMEM((rows, channels), jnp.float32),
            pltpu.VMEM((OFFSETS, rows, 128), jnp.float32),
            pltpu.VMEM((rows, channels), jnp.float32),
            pltpu.VMEM((rows, 128), jnp.float32),
            dma((4,)),
            dma((ticks, SLOTS)),
            dma((5, OFFSETS)),
            dma((OFFSETS,)),
            dma((OFFSETS,)),
        ],
        compiler_params=pltpu.CompilerParams(collective_id=0, has_side_effects=True),
    )(features, select, validity, offset_gain)


def solution(mesh):
    in_specs = (P("sec", "tile", None), P("sec", "tile"), P("sec"), P())
    out_specs = P("sec", "tile", None)
    return jax.shard_map(shards, mesh=mesh, in_specs=in_specs, out_specs=out_specs, check_vma=False)
```

```python
import functools
import math

import jax
import jax.numpy as jnp
from jax import lax
from jax.experimental import pallas as pl
from jax.experimental.pallas import tpu as pltpu
from jax.sharding import PartitionSpec as P

MESH = pl.DeviceIdType.MESH
OFFSETS = 3
LENGTH_Z = 8
LENGTH_Y = 4
LENGTH_X = 4
PIECES = 8
GROUP = 2
SIDE_LAG = 6
MATCH_LAG = 8
SLOTS = 5
ROW_BLOCK = 256
score_factor = 2.5


def device_at(x, y, z, core):
    return ((x * 2 + y % 2) * LENGTH_Z + z, (y // 2) * 2 + core)


def lane_sum(weights):
    lanes = [weights[:, lane : lane + 128] for lane in range(0, weights.shape[1], 128)]
    while len(lanes) > 1:
        lanes = [a + b for a, b in zip(lanes[::2], lanes[1::2])]
    return lanes[0]


def kernel(
    features,
    select,
    validity,
    gain,
    out,
    keys,
    queries,
    votes_in,
    gains,
    own_flag,
    flags,
    high,
    total,
    weighted,
    chosen,
    numerator,
    count,
    local_sem,
    arrive,
    sent,
    flag_arrive,
    flag_sent,
):
    rows, channels = queries.shape
    ticks = OFFSETS * PIECES
    groups = PIECES // GROUP
    sections = lax.axis_size("sec")
    piece = rows // PIECES
    to_exponent = score_factor / math.sqrt(channels) * math.log2(math.e)

    section, tile = lax.axis_index("sec"), lax.axis_index("tile")
    z = section % LENGTH_Z
    x = section // (2 * LENGTH_Z)
    y = (tile // 2) * 2 + (section // LENGTH_Z) % 2
    core = tile % 2
    first = z == 0
    odd = y % 2
    last_z = z == LENGTH_Z - 1
    sends_up = section < sections - 1

    def crosses(offset):
        return offset >= z

    def comes_up(offset):
        return jnp.logical_not(jnp.logical_and(jnp.logical_and(x == 0, odd == 1), crosses(offset)))

    def usable_offset(offset):
        return section > offset

    up = device_at(
        jnp.where(last_z, (x + odd) % LENGTH_X, x), y, (z + 1) % LENGTH_Z, core
    )
    down = device_at(
        jnp.where(first, (x + LENGTH_X - odd) % LENGTH_X, x), y, (z + LENGTH_Z - 1) % LENGTH_Z, core
    )
    partner = device_at(x, y, z, 1 - core)
    pair = device_at(x, (y + 2) % LENGTH_Y, z, core)
    right = device_at(x, (y + 1) % LENGTH_Y, z, core)
    left = device_at(x, (y + 3) % LENGTH_Y, z, core)

    copy_queries = pltpu.make_async_copy(features.at[0], queries, local_sem.at[0])
    copy_votes = pltpu.make_async_copy(select, votes_in, local_sem.at[1])
    copy_gains = pltpu.make_async_copy(gain, gains, local_sem.at[2])
    copy_flag = pltpu.make_async_copy(validity, own_flag, local_sem.at[3])
    copy_flag.start()
    copy_queries.start()
    copy_votes.start()
    copy_gains.start()

    barrier = pltpu.get_barrier_semaphore()

    def greet(target):
        pl.semaphore_signal(barrier, inc=1, device_id=target, device_id_type=MESH)

    greet(down)
    greet(partner)
    for offset in range(OFFSETS):
        greet(((section + sections - offset - 1) % sections, tile))

    @pl.when(z < OFFSETS)
    def _():
        greet(left)
        greet(right)

    @pl.when(z > 0)
    def _():
        greet(pair)

    copy_votes.wait()
    copy_gains.wait()
    picks = jnp.broadcast_to(votes_in[...], (128, rows)).T
    for offset in range(OFFSETS):
        chosen[offset] = (picks // 2**offset % 2).astype(jnp.float32)
    numerator[...] = jnp.zeros_like(numerator)
    count[...] = jnp.zeros_like(count)
    pl.semaphore_wait(barrier, 2 + OFFSETS + jnp.where(z < OFFSETS, 2, 0) + jnp.where(z > 0, 1, 0))

    def send(source, tick, slot, sem, target):
        return pltpu.make_async_remote_copy(
            src_ref=source,
            dst_ref=keys.at[tick, slot],
            send_sem=sem,
            recv_sem=arrive.at[tick, slot],
            device_id=target,
            device_id_type=MESH,
        )

    def own_piece(j):
        return features.at[0, pl.ds(j * piece, piece)]

    def send_flag(offset):
        return pltpu.make_async_remote_copy(
            src_ref=own_flag,
            dst_ref=flags.at[offset],
            send_sem=flag_sent.at[offset],
            recv_sem=flag_arrive.at[offset],
            device_id=((section + offset + 1) % sections, tile),
            device_id_type=MESH,
        )

    copy_flag.wait()
    for offset in range(OFFSETS):
        send_flag(offset).start()

    @pl.when(sends_up)
    def _():
        for j in range(PIECES):
            send(own_piece(j), j, 0, sent.at[0, 0], up).start()

    copy_queries.wait()

    def wait_for(tick, slot):
        pltpu.make_async_copy(keys.at[tick, slot], keys.at[tick, slot], arrive.at[tick, slot]).wait()

    def take_from_below(i):
        offset = i // PIECES

        @pl.when(comes_up(offset))
        def _():
            wait_for(i, 0)

            @pl.when(jnp.logical_and(sends_up, offset < OFFSETS - 1))
            def _():
                send(keys.at[i, 0], i + PIECES, 0, sent.at[0, offset + 1], up).start()

            @pl.when(crosses(offset))
            def _():
                send(keys.at[i, 0], i, 4, sent.at[1, offset], right).start()
                send(keys.at[i, 0], i, 1, sent.at[2, offset], left).start()

            @pl.when(jnp.logical_not(crosses(offset)))
            def _():
                send(keys.at[i, 0], i, 1, sent.at[1, offset], pair).start()
                send(keys.at[i, 0], i, 2, sent.at[3, offset], partner).start()

    def take_from_side(i):
        offset = i // PIECES

        @pl.when(usable_offset(offset))
        def _():
            @pl.when(crosses(offset))
            def _():
                wait_for(i, 4)
                send(keys.at[i, 4], i, 2, sent.at[3, offset], partner).start()

            wait_for(i, 1)
            send(keys.at[i, 1], i, 3, sent.at[4, offset], partner).start()

    def flag_wait(offset):
        pltpu.make_async_copy(flags.at[offset], flags.at[offset], flag_arrive.at[offset]).wait()

    def match(g):
        for k in range(GROUP):
            wait_for(g * GROUP + k, 2)
            wait_for(g * GROUP + k, 3)
        offset = g // groups
        start = jnp.where(crosses(offset), 1, 0)

        @pl.when(g % groups == 0)
        def _():
            high[...] = jnp.full_like(high, -1e30)
            total[...] = jnp.zeros_like(total)
            weighted[...] = jnp.zeros_like(weighted)

        key_rows = keys[pl.ds(g * GROUP, GROUP), pl.ds(start, 4)].reshape(GROUP * 4 * piece, channels)
        parts = [pl.ds(block * ROW_BLOCK, ROW_BLOCK) for block in range(rows // ROW_BLOCK)]
        scores = [
            lax.dot_general(
                queries[part], key_rows, (((1,), (1,)), ((), ())), preferred_element_type=jnp.float32
            )
            for part in parts
        ]
        rounded, fades = [], []
        for part, block in zip(parts, scores):
            before = high[part]
            now = jnp.maximum(before, jnp.max(block, axis=1, keepdims=True) * to_exponent)
            weights = jnp.exp2(block * to_exponent - now[:, :1])
            fade = jnp.exp2(before - now)
            total[part] = fade * total[part] + lane_sum(weights)
            high[part] = now
            rounded.append(weights.astype(jnp.bfloat16))
            fades.append(jnp.concatenate([fade, fade], axis=1))
        for part, weights, fade in zip(parts, rounded, fades):
            weighted[part] = fade * weighted[part] + jnp.dot(
                weights, key_rows, preferred_element_type=jnp.float32
            )

        @pl.when(g % groups == groups - 1)
        def _():
            flag_wait(offset)
            usable = flags[offset, 0].astype(jnp.float32)
            vote = chosen[pl.ds(offset, 1)][0] * usable
            count[...] += vote
            factor = vote[:, :1] / jnp.sum(total[...], axis=1, keepdims=True)
            numerator[...] += factor * gains[pl.ds(offset, 1)] * weighted[...]

    def step(i, carry):
        @pl.when(i < ticks)
        def _():
            take_from_below(i)

        @pl.when(jnp.logical_and(i >= SIDE_LAG, i < ticks + SIDE_LAG))
        def _():
            take_from_side(i - SIDE_LAG)

        @pl.when(jnp.logical_and(i >= MATCH_LAG + GROUP - 1, (i - MATCH_LAG) % GROUP == GROUP - 1))
        def _():
            g = (i - MATCH_LAG) // GROUP

            @pl.when(usable_offset(g // groups))
            def _():
                match(g)

        return carry

    lax.fori_loop(0, ticks + MATCH_LAG, step, 0)

    out[0] = (numerator[...] / jnp.maximum(count[...], 1.0)[:, :1]).astype(jnp.bfloat16)

    def wait_sent(kind, offset, sends):
        @pl.when(sends)
        def _():
            tile_sent = keys.at[pl.ds(0, PIECES), 0]
            pltpu.make_async_copy(tile_sent, tile_sent, sent.at[kind, offset]).wait()

    wait_sent(0, 0, sends_up)
    for offset in range(OFFSETS):
        if offset > 0:
            wait_sent(0, offset, jnp.logical_and(sends_up, comes_up(offset - 1)))
        wait_sent(1, offset, comes_up(offset))
        wait_sent(2, offset, jnp.logical_and(comes_up(offset), crosses(offset)))
        wait_sent(3, offset, usable_offset(offset))
        wait_sent(4, offset, usable_offset(offset))

    for offset in range(OFFSETS):
        @pl.when(jnp.logical_not(usable_offset(offset)))
        def _():
            flag_wait(offset)

        send_flag(offset).wait_send()


def in_hbm(array):
    return pltpu.with_memory_space_constraint(array, pltpu.HBM)


def shards(features, select, validity, offset_gain):
    rows, channels = features.shape[1:]
    ticks = OFFSETS * PIECES
    anywhere = pl.BlockSpec(memory_space=pltpu.HBM)
    dma = pltpu.SemaphoreType.DMA
    return pl.pallas_call(
        kernel,
        out_shape=jax.ShapeDtypeStruct(features.shape, jnp.bfloat16),
        in_specs=[anywhere] * 4,
        out_specs=pl.BlockSpec(memory_space=pltpu.VMEM),
        scratch_shapes=[
            pltpu.VMEM((ticks, SLOTS, rows // PIECES, channels), jnp.bfloat16),
            pltpu.VMEM((rows, channels), jnp.bfloat16),
            pltpu.VMEM(select.shape, jnp.int32),
            pltpu.VMEM(offset_gain.shape, jnp.float32),
            pltpu.SMEM((1,), jnp.int32),
            pltpu.SMEM((OFFSETS, 1), jnp.int32),
            pltpu.VMEM((rows, 128), jnp.float32),
            pltpu.VMEM((rows, 128), jnp.float32),
            pltpu.VMEM((rows, channels), jnp.float32),
            pltpu.VMEM((OFFSETS, rows, 128), jnp.float32),
            pltpu.VMEM((rows, channels), jnp.float32),
            pltpu.VMEM((rows, 128), jnp.float32),
            dma((4,)),
            dma((ticks, SLOTS)),
            dma((5, OFFSETS)),
            dma((OFFSETS,)),
            dma((OFFSETS,)),
        ],
        compiler_params=pltpu.CompilerParams(collective_id=0, has_side_effects=True, vmem_limit_bytes=20 << 20),
    )(in_hbm(features), in_hbm(select), validity, in_hbm(offset_gain))


def solution(mesh):
    in_specs = (P("sec", "tile", None), P("sec", "tile"), P("sec"), P())
    out_specs = P("sec", "tile", None)
    return jax.shard_map(shards, mesh=mesh, in_specs=in_specs, out_specs=out_specs, check_vma=False)
```

```python
import functools
import math

import jax
import jax.numpy as jnp
from jax import lax
from jax.experimental import pallas as pl
from jax.experimental.pallas import tpu as pltpu
from jax.sharding import PartitionSpec as P

MESH = pl.DeviceIdType.MESH
OFFSETS = 3
LENGTH_Z = 8
LENGTH_Y = 4
LENGTH_X = 4
PIECES = 4
GROUP = 1
SIDE_LAG = 4
MATCH_LAG = 5
SLOTS = 5
ROW_BLOCK = 256
score_factor = 2.5


def device_at(x, y, z, core):
    return ((x * 2 + y % 2) * LENGTH_Z + z, (y // 2) * 2 + core)


def lane_sum(weights):
    lanes = [weights[:, lane : lane + 128] for lane in range(0, weights.shape[1], 128)]
    while len(lanes) > 1:
        lanes = [a + b for a, b in zip(lanes[::2], lanes[1::2])]
    return lanes[0]


def kernel(
    features,
    select,
    validity,
    gain,
    out,
    keys,
    queries,
    votes_in,
    gains,
    own_flag,
    flags,
    high,
    total,
    weighted,
    chosen,
    numerator,
    count,
    local_sem,
    arrive,
    sent,
    flag_arrive,
    flag_sent,
):
    rows, channels = queries.shape
    ticks = OFFSETS * PIECES
    groups = PIECES // GROUP
    sections = lax.axis_size("sec")
    piece = rows // PIECES
    to_exponent = score_factor / math.sqrt(channels) * math.log2(math.e)

    section, tile = lax.axis_index("sec"), lax.axis_index("tile")
    z = section % LENGTH_Z
    x = section // (2 * LENGTH_Z)
    y = (tile // 2) * 2 + (section // LENGTH_Z) % 2
    core = tile % 2
    first = z == 0
    odd = y % 2
    last_z = z == LENGTH_Z - 1
    sends_up = section < sections - 1

    def crosses(offset):
        return offset >= z

    def comes_up(offset):
        return jnp.logical_not(jnp.logical_and(jnp.logical_and(x == 0, odd == 1), crosses(offset)))

    def usable_offset(offset):
        return section > offset

    up = device_at(
        jnp.where(last_z, (x + odd) % LENGTH_X, x), y, (z + 1) % LENGTH_Z, core
    )
    down = device_at(
        jnp.where(first, (x + LENGTH_X - odd) % LENGTH_X, x), y, (z + LENGTH_Z - 1) % LENGTH_Z, core
    )
    partner = device_at(x, y, z, 1 - core)
    pair = device_at(x, (y + 2) % LENGTH_Y, z, core)
    right = device_at(x, (y + 1) % LENGTH_Y, z, core)
    left = device_at(x, (y + 3) % LENGTH_Y, z, core)

    copy_queries = pltpu.make_async_copy(features.at[0], queries, local_sem.at[0])
    copy_votes = pltpu.make_async_copy(select, votes_in, local_sem.at[1])
    copy_gains = pltpu.make_async_copy(gain, gains, local_sem.at[2])
    copy_flag = pltpu.make_async_copy(validity, own_flag, local_sem.at[3])
    copy_flag.start()
    copy_queries.start()
    copy_votes.start()
    copy_gains.start()

    barrier = pltpu.get_barrier_semaphore()

    def greet(target):
        pl.semaphore_signal(barrier, inc=1, device_id=target, device_id_type=MESH)

    greet(down)
    greet(partner)
    for offset in range(OFFSETS):
        greet(((section + sections - offset - 1) % sections, tile))

    @pl.when(z < OFFSETS)
    def _():
        greet(left)
        greet(right)

    @pl.when(z > 0)
    def _():
        greet(pair)

    copy_votes.wait()
    copy_gains.wait()
    picks = jnp.broadcast_to(votes_in[...], (128, rows)).T
    for offset in range(OFFSETS):
        chosen[offset] = (picks // 2**offset % 2).astype(jnp.float32)
    numerator[...] = jnp.zeros_like(numerator)
    count[...] = jnp.zeros_like(count)
    pl.semaphore_wait(barrier, 2 + OFFSETS + jnp.where(z < OFFSETS, 2, 0) + jnp.where(z > 0, 1, 0))

    def send(source, tick, slot, sem, target):
        return pltpu.make_async_remote_copy(
            src_ref=source,
            dst_ref=keys.at[tick, slot],
            send_sem=sem,
            recv_sem=arrive.at[tick, slot],
            device_id=target,
            device_id_type=MESH,
        )

    def own_piece(j):
        return features.at[0, pl.ds(j * piece, piece)]

    def send_flag(offset):
        return pltpu.make_async_remote_copy(
            src_ref=own_flag,
            dst_ref=flags.at[offset],
            send_sem=flag_sent.at[offset],
            recv_sem=flag_arrive.at[offset],
            device_id=((section + offset + 1) % sections, tile),
            device_id_type=MESH,
        )

    copy_flag.wait()

    @pl.when(sends_up)
    def _():
        for j in range(PIECES):
            send(own_piece(j), j, 0, sent.at[0, 0], up).start()

    for offset in range(OFFSETS):
        send_flag(offset).start()
    copy_queries.wait()

    def wait_for(tick, slot):
        pltpu.make_async_copy(keys.at[tick, slot], keys.at[tick, slot], arrive.at[tick, slot]).wait()

    def take_from_below(i):
        offset = i // PIECES

        @pl.when(comes_up(offset))
        def _():
            wait_for(i, 0)

            @pl.when(crosses(offset))
            def _():
                send(keys.at[i, 0], i, 4, sent.at[1, offset], right).start()
                send(keys.at[i, 0], i, 1, sent.at[2, offset], left).start()

            @pl.when(jnp.logical_not(crosses(offset)))
            def _():
                send(keys.at[i, 0], i, 1, sent.at[1, offset], pair).start()
                send(keys.at[i, 0], i, 2, sent.at[3, offset], partner).start()

            @pl.when(jnp.logical_and(sends_up, offset < OFFSETS - 1))
            def _():
                send(keys.at[i, 0], i + PIECES, 0, sent.at[0, offset + 1], up).start()

    def take_from_side(i):
        offset = i // PIECES

        @pl.when(usable_offset(offset))
        def _():
            @pl.when(crosses(offset))
            def _():
                wait_for(i, 4)
                send(keys.at[i, 4], i, 2, sent.at[3, offset], partner).start()

            wait_for(i, 1)
            send(keys.at[i, 1], i, 3, sent.at[4, offset], partner).start()

    def flag_wait(offset):
        pltpu.make_async_copy(flags.at[offset], flags.at[offset], flag_arrive.at[offset]).wait()

    def match(g):
        for k in range(GROUP):
            wait_for(g * GROUP + k, 2)
            wait_for(g * GROUP + k, 3)
        offset = g // groups
        start = jnp.where(crosses(offset), 1, 0)

        @pl.when(g % groups == 0)
        def _():
            high[...] = jnp.full_like(high, -1e30)
            total[...] = jnp.zeros_like(total)
            weighted[...] = jnp.zeros_like(weighted)

        key_rows = keys[pl.ds(g * GROUP, GROUP), pl.ds(start, 4)].reshape(GROUP * 4 * piece, channels)
        parts = [pl.ds(block * ROW_BLOCK, ROW_BLOCK) for block in range(rows // ROW_BLOCK)]
        scores = [
            lax.dot_general(
                queries[part], key_rows, (((1,), (1,)), ((), ())), preferred_element_type=jnp.float32
            )
            for part in parts
        ]
        rounded, fades = [], []
        for part, block in zip(parts, scores):
            before = high[part]
            now = jnp.maximum(before, jnp.max(block, axis=1, keepdims=True) * to_exponent)
            weights = jnp.exp2(block * to_exponent - now[:, :1])
            fade = jnp.exp2(before - now)
            total[part] = fade * total[part] + lane_sum(weights)
            high[part] = now
            rounded.append(weights.astype(jnp.bfloat16))
            fades.append(jnp.concatenate([fade, fade], axis=1))
        for part, weights, fade in zip(parts, rounded, fades):
            weighted[part] = fade * weighted[part] + jnp.dot(
                weights, key_rows, preferred_element_type=jnp.float32
            )

        @pl.when(g % groups == groups - 1)
        def _():
            flag_wait(offset)
            usable = flags[offset, 0].astype(jnp.float32)
            vote = chosen[pl.ds(offset, 1)][0] * usable
            count[...] += vote
            factor = vote[:, :1] / jnp.sum(total[...], axis=1, keepdims=True)
            result = numerator[...] + factor * gains[pl.ds(offset, 1)] * weighted[...]

            @pl.when(offset < OFFSETS - 1)
            def _():
                numerator[...] = result

            @pl.when(offset == OFFSETS - 1)
            def _():
                out[0] = (result / jnp.maximum(count[...], 1.0)[:, :1]).astype(jnp.bfloat16)

    def step(i, carry):
        @pl.when(i < ticks)
        def _():
            take_from_below(i)

        @pl.when(jnp.logical_and(i >= SIDE_LAG, i < ticks + SIDE_LAG))
        def _():
            take_from_side(i - SIDE_LAG)

        @pl.when(jnp.logical_and(i >= MATCH_LAG + GROUP - 1, (i - MATCH_LAG) % GROUP == GROUP - 1))
        def _():
            g = (i - MATCH_LAG) // GROUP

            @pl.when(usable_offset(g // groups))
            def _():
                match(g)

        return carry

    lax.fori_loop(0, ticks + MATCH_LAG, step, 0)

    @pl.when(jnp.logical_not(usable_offset(OFFSETS - 1)))
    def _():
        out[0] = (numerator[...] / jnp.maximum(count[...], 1.0)[:, :1]).astype(jnp.bfloat16)

    def wait_sent(kind, offset, sends):
        @pl.when(sends)
        def _():
            tile_sent = keys.at[pl.ds(0, PIECES), 0]
            pltpu.make_async_copy(tile_sent, tile_sent, sent.at[kind, offset]).wait()

    wait_sent(0, 0, sends_up)
    for offset in range(OFFSETS):
        if offset > 0:
            wait_sent(0, offset, jnp.logical_and(sends_up, comes_up(offset - 1)))
        wait_sent(1, offset, comes_up(offset))
        wait_sent(2, offset, jnp.logical_and(comes_up(offset), crosses(offset)))
        wait_sent(3, offset, usable_offset(offset))
        wait_sent(4, offset, usable_offset(offset))

    for offset in range(OFFSETS):
        @pl.when(jnp.logical_not(usable_offset(offset)))
        def _():
            flag_wait(offset)

        send_flag(offset).wait_send()


def in_hbm(array):
    return pltpu.with_memory_space_constraint(array, pltpu.HBM)


def shards(features, select, validity, offset_gain):
    rows, channels = features.shape[1:]
    ticks = OFFSETS * PIECES
    anywhere = pl.BlockSpec(memory_space=pltpu.HBM)
    dma = pltpu.SemaphoreType.DMA
    return pl.pallas_call(
        kernel,
        out_shape=jax.ShapeDtypeStruct(features.shape, jnp.bfloat16),
        in_specs=[anywhere] * 4,
        out_specs=pl.BlockSpec(memory_space=pltpu.VMEM),
        scratch_shapes=[
            pltpu.VMEM((ticks, SLOTS, rows // PIECES, channels), jnp.bfloat16),
            pltpu.VMEM((rows, channels), jnp.bfloat16),
            pltpu.VMEM(select.shape, jnp.int32),
            pltpu.VMEM(offset_gain.shape, jnp.float32),
            pltpu.SMEM((1,), jnp.int32),
            pltpu.SMEM((OFFSETS, 1), jnp.int32),
            pltpu.VMEM((rows, 128), jnp.float32),
            pltpu.VMEM((rows, 128), jnp.float32),
            pltpu.VMEM((rows, channels), jnp.float32),
            pltpu.VMEM((OFFSETS, rows, 128), jnp.float32),
            pltpu.VMEM((rows, channels), jnp.float32),
            pltpu.VMEM((rows, 128), jnp.float32),
            dma((4,)),
            dma((ticks, SLOTS)),
            dma((5, OFFSETS)),
            dma((OFFSETS,)),
            dma((OFFSETS,)),
        ],
        compiler_params=pltpu.CompilerParams(collective_id=0, has_side_effects=True, vmem_limit_bytes=20 << 20),
    )(in_hbm(features), in_hbm(select), validity, in_hbm(offset_gain))


def solution(mesh):
    in_specs = (P("sec", "tile", None), P("sec", "tile"), P("sec"), P())
    out_specs = P("sec", "tile", None)
    return jax.shard_map(shards, mesh=mesh, in_specs=in_specs, out_specs=out_specs, check_vma=False)
```

```python
import functools
import math

import jax
import jax.numpy as jnp
from jax import lax
from jax.experimental import pallas as pl
from jax.experimental.pallas import tpu as pltpu
from jax.sharding import PartitionSpec as P

MESH = pl.DeviceIdType.MESH
OFFSETS = 3
LENGTH_Z = 8
LENGTH_Y = 4
LENGTH_X = 4
PIECES = 4
GROUP = 1
SIDE_LAG = 4
MATCH_LAG = 5
SLOTS = 5
ROW_BLOCK = 256
score_factor = 2.5


def device_at(x, y, z, core):
    return ((x * 2 + y % 2) * LENGTH_Z + z, (y // 2) * 2 + core)


def lane_sum(weights):
    lanes = [weights[:, lane : lane + 128] for lane in range(0, weights.shape[1], 128)]
    while len(lanes) > 1:
        lanes = [a + b for a, b in zip(lanes[::2], lanes[1::2])]
    return lanes[0]


def kernel(
    features,
    select,
    validity,
    gain,
    out,
    keys,
    queries,
    votes_in,
    gains,
    own_flag,
    flags,
    high,
    total,
    weighted,
    chosen,
    numerator,
    count,
    local_sem,
    arrive,
    sent,
    flag_arrive,
    flag_sent,
):
    rows, channels = queries.shape
    ticks = OFFSETS * PIECES
    groups = PIECES // GROUP
    sections = lax.axis_size("sec")
    piece = rows // PIECES
    to_exponent = score_factor / math.sqrt(channels) * math.log2(math.e)

    section, tile = lax.axis_index("sec"), lax.axis_index("tile")
    z = section % LENGTH_Z
    x = section // (2 * LENGTH_Z)
    y = (tile // 2) * 2 + (section // LENGTH_Z) % 2
    core = tile % 2
    first = z == 0
    odd = y % 2
    last_z = z == LENGTH_Z - 1
    sends_up = section < sections - 1

    def crosses(offset):
        return offset >= z

    def comes_up(offset):
        return jnp.logical_not(jnp.logical_and(jnp.logical_and(x == 0, odd == 1), crosses(offset)))

    def usable_offset(offset):
        return section > offset

    up = device_at(
        jnp.where(last_z, (x + odd) % LENGTH_X, x), y, (z + 1) % LENGTH_Z, core
    )
    down = device_at(
        jnp.where(first, (x + LENGTH_X - odd) % LENGTH_X, x), y, (z + LENGTH_Z - 1) % LENGTH_Z, core
    )
    partner = device_at(x, y, z, 1 - core)
    pair = device_at(x, (y + 2) % LENGTH_Y, z, core)
    right = device_at(x, (y + 1) % LENGTH_Y, z, core)
    left = device_at(x, (y + 3) % LENGTH_Y, z, core)

    copy_queries = pltpu.make_async_copy(features.at[0], queries, local_sem.at[0])
    copy_votes = pltpu.make_async_copy(select, votes_in, local_sem.at[1])
    copy_gains = pltpu.make_async_copy(gain, gains, local_sem.at[2])
    copy_flag = pltpu.make_async_copy(validity, own_flag, local_sem.at[3])
    copy_flag.start()
    copy_queries.start()
    copy_votes.start()
    copy_gains.start()

    barrier = pltpu.get_barrier_semaphore()

    def greet(target):
        pl.semaphore_signal(barrier, inc=1, device_id=target, device_id_type=MESH)

    greet(down)
    greet(partner)
    for offset in range(OFFSETS):
        greet(((section + sections - offset - 1) % sections, tile))

    @pl.when(z < OFFSETS)
    def _():
        greet(left)
        greet(right)

    @pl.when(z > 0)
    def _():
        greet(pair)

    copy_votes.wait()
    copy_gains.wait()
    picks = jnp.broadcast_to(votes_in[...], (128, rows)).T
    for offset in range(OFFSETS):
        chosen[offset] = (picks // 2**offset % 2).astype(jnp.float32)
    numerator[...] = jnp.zeros_like(numerator)
    count[...] = jnp.zeros_like(count)
    pl.semaphore_wait(barrier, 2 + OFFSETS + jnp.where(z < OFFSETS, 2, 0) + jnp.where(z > 0, 1, 0))

    def send(source, tick, slot, sem, target):
        return pltpu.make_async_remote_copy(
            src_ref=source,
            dst_ref=keys.at[tick, slot],
            send_sem=sem,
            recv_sem=arrive.at[tick, slot],
            device_id=target,
            device_id_type=MESH,
        )

    def own_piece(j):
        return features.at[0, pl.ds(j * piece, piece)]

    def send_flag(offset):
        return pltpu.make_async_remote_copy(
            src_ref=own_flag,
            dst_ref=flags.at[offset],
            send_sem=flag_sent.at[offset],
            recv_sem=flag_arrive.at[offset],
            device_id=((section + offset + 1) % sections, tile),
            device_id_type=MESH,
        )

    copy_flag.wait()

    @pl.when(sends_up)
    def _():
        for j in range(PIECES):
            send(own_piece(j), j, 0, sent.at[0, 0], up).start()

    for offset in range(OFFSETS):
        send_flag(offset).start()
    copy_queries.wait()

    def wait_for(tick, slot):
        pltpu.make_async_copy(keys.at[tick, slot], keys.at[tick, slot], arrive.at[tick, slot]).wait()

    def take_from_below(i):
        offset = i // PIECES

        @pl.when(comes_up(offset))
        def _():
            wait_for(i, 0)

            @pl.when(crosses(offset))
            def _():
                send(keys.at[i, 0], i, 4, sent.at[1, offset], right).start()
                send(keys.at[i, 0], i, 1, sent.at[2, offset], left).start()

            @pl.when(jnp.logical_not(crosses(offset)))
            def _():
                send(keys.at[i, 0], i, 1, sent.at[1, offset], pair).start()
                send(keys.at[i, 0], i, 2, sent.at[3, offset], partner).start()

            @pl.when(jnp.logical_and(sends_up, offset < OFFSETS - 1))
            def _():
                send(keys.at[i, 0], i + PIECES, 0, sent.at[0, offset + 1], up).start()

    def take_from_side(i):
        offset = i // PIECES

        @pl.when(usable_offset(offset))
        def _():
            @pl.when(crosses(offset))
            def _():
                wait_for(i, 4)
                send(keys.at[i, 4], i, 2, sent.at[3, offset], partner).start()

            wait_for(i, 1)
            send(keys.at[i, 1], i, 3, sent.at[4, offset], partner).start()

    def flag_wait(offset):
        pltpu.make_async_copy(flags.at[offset], flags.at[offset], flag_arrive.at[offset]).wait()

    def match(g):
        for k in range(GROUP):
            wait_for(g * GROUP + k, 2)
            wait_for(g * GROUP + k, 3)
        offset = g // groups
        start = jnp.where(crosses(offset), 1, 0)

        @pl.when(g % groups == 0)
        def _():
            high[...] = jnp.full_like(high, -1e30)
            total[...] = jnp.zeros_like(total)
            weighted[...] = jnp.zeros_like(weighted)

        key_rows = keys[pl.ds(g * GROUP, GROUP), pl.ds(start, 4)].reshape(GROUP * 4 * piece, channels)
        parts = [pl.ds(block * ROW_BLOCK, ROW_BLOCK) for block in range(rows // ROW_BLOCK)]
        scores = [
            lax.dot_general(
                queries[part], key_rows, (((1,), (1,)), ((), ())), preferred_element_type=jnp.float32
            )
            for part in parts
        ]
        rounded, fades = [], []
        for part, block in zip(parts, scores):
            before = high[part]
            now = jnp.maximum(before, jnp.max(block, axis=1, keepdims=True))
            weights = jnp.exp2((block - now[:, :1]) * to_exponent)
            fade = jnp.exp2((before - now) * to_exponent)
            total[part] = fade * total[part] + lane_sum(weights)
            high[part] = now
            rounded.append(weights.astype(jnp.bfloat16))
            fades.append(jnp.concatenate([fade, fade], axis=1))
        for part, weights, fade in zip(parts, rounded, fades):
            weighted[part] = fade * weighted[part] + jnp.dot(
                weights, key_rows, preferred_element_type=jnp.float32
            )

        @pl.when(g % groups == groups - 1)
        def _():
            flag_wait(offset)
            usable = flags[offset, 0].astype(jnp.float32)
            vote = chosen[pl.ds(offset, 1)][0] * usable
            count[...] += vote
            factor = vote[:, :1] / jnp.sum(total[...], axis=1, keepdims=True)
            result = numerator[...] + factor * gains[pl.ds(offset, 1)] * weighted[...]

            @pl.when(offset < OFFSETS - 1)
            def _():
                numerator[...] = result

            @pl.when(offset == OFFSETS - 1)
            def _():
                out[0] = (result / jnp.maximum(count[...], 1.0)[:, :1]).astype(jnp.bfloat16)

    def step(i, carry):
        @pl.when(i < ticks)
        def _():
            take_from_below(i)

        @pl.when(jnp.logical_and(i >= SIDE_LAG, i < ticks + SIDE_LAG))
        def _():
            take_from_side(i - SIDE_LAG)

        @pl.when(jnp.logical_and(i >= MATCH_LAG + GROUP - 1, (i - MATCH_LAG) % GROUP == GROUP - 1))
        def _():
            g = (i - MATCH_LAG) // GROUP

            @pl.when(usable_offset(g // groups))
            def _():
                match(g)

        return carry

    lax.fori_loop(0, ticks + MATCH_LAG, step, 0)

    @pl.when(jnp.logical_not(usable_offset(OFFSETS - 1)))
    def _():
        out[0] = (numerator[...] / jnp.maximum(count[...], 1.0)[:, :1]).astype(jnp.bfloat16)

    def wait_sent(kind, offset, sends):
        @pl.when(sends)
        def _():
            tile_sent = keys.at[pl.ds(0, PIECES), 0]
            pltpu.make_async_copy(tile_sent, tile_sent, sent.at[kind, offset]).wait()

    wait_sent(0, 0, sends_up)
    for offset in range(OFFSETS):
        if offset > 0:
            wait_sent(0, offset, jnp.logical_and(sends_up, comes_up(offset - 1)))
        wait_sent(1, offset, comes_up(offset))
        wait_sent(2, offset, jnp.logical_and(comes_up(offset), crosses(offset)))
        wait_sent(3, offset, usable_offset(offset))
        wait_sent(4, offset, usable_offset(offset))

    for offset in range(OFFSETS):
        @pl.when(jnp.logical_not(usable_offset(offset)))
        def _():
            flag_wait(offset)

        send_flag(offset).wait_send()


def in_hbm(array):
    return pltpu.with_memory_space_constraint(array, pltpu.HBM)


def shards(features, select, validity, offset_gain):
    rows, channels = features.shape[1:]
    ticks = OFFSETS * PIECES
    anywhere = pl.BlockSpec(memory_space=pltpu.HBM)
    dma = pltpu.SemaphoreType.DMA
    return pl.pallas_call(
        kernel,
        out_shape=jax.ShapeDtypeStruct(features.shape, jnp.bfloat16),
        in_specs=[anywhere] * 4,
        out_specs=pl.BlockSpec(memory_space=pltpu.VMEM),
        scratch_shapes=[
            pltpu.VMEM((ticks, SLOTS, rows // PIECES, channels), jnp.bfloat16),
            pltpu.VMEM((rows, channels), jnp.bfloat16),
            pltpu.VMEM(select.shape, jnp.int32),
            pltpu.VMEM(offset_gain.shape, jnp.float32),
            pltpu.SMEM((1,), jnp.int32),
            pltpu.SMEM((OFFSETS, 1), jnp.int32),
            pltpu.VMEM((rows, 128), jnp.float32),
            pltpu.VMEM((rows, 128), jnp.float32),
            pltpu.VMEM((rows, channels), jnp.float32),
            pltpu.VMEM((OFFSETS, rows, 128), jnp.float32),
            pltpu.VMEM((rows, channels), jnp.float32),
            pltpu.VMEM((rows, 128), jnp.float32),
            dma((4,)),
            dma((ticks, SLOTS)),
            dma((5, OFFSETS)),
            dma((OFFSETS,)),
            dma((OFFSETS,)),
        ],
        compiler_params=pltpu.CompilerParams(collective_id=0, has_side_effects=True, vmem_limit_bytes=20 << 20),
    )(in_hbm(features), in_hbm(select), validity, in_hbm(offset_gain))


def solution(mesh):
    in_specs = (P("sec", "tile", None), P("sec", "tile"), P("sec"), P())
    out_specs = P("sec", "tile", None)
    return jax.shard_map(shards, mesh=mesh, in_specs=in_specs, out_specs=out_specs, check_vma=False)
```
